32 devices in a mesh: dp: 2 (over x), row: 4 (over y, core), col: 4 (over z).
Axes of the slice: x: 2, y: 2, z: 4, core: 2. Of those that a mesh axis runs over, the one named last changes fastest.
Arguments:
- tokens: bfloat16 [16, 577, 1024], P(('dp', 'row'), None, 'col'), may hold values from -6 to 6
- cotangent: bfloat16 [16, 577, 1024], P(('dp', 'row'), None, 'col'), may hold values from -6 to 6
- w_qkv: bfloat16 [1024, 3, 1024], P('row', None, 'col'), may hold values from -0.1875 to 0.1875
- b_qv: float32 [2, 1024], P(None, 'col'), may hold values from -3 to 3
- w_out: bfloat16 [1024, 1024], P('row', 'col'), may hold values from -0.75 to 0.75
- b_out: float32 [1024], P('col'), may hold values from -3 to 3
- g_one: float32 [1024], P('col'), may hold values from 0.1 to 1.9
- c_one: float32 [1024], P('col'), may hold values from -3 to 3
- w_up: bfloat16 [1024, 4096], P('row', 'col'), may hold values from -0.1875 to 0.1875
- b_up: float32 [4096], P('col'), may hold values from -3 to 3
- w_down: bfloat16 [4096, 1024], P('row', 'col'), may hold values from -0.09375 to 0.09375
- b_down: float32 [1024], P('col'), may hold values from -3 to 3
- g_two: float32 [1024], P('col'), may hold values from 0.1 to 1.9
- c_two: float32 [1024], P('col'), may hold values from -3 to 3
Outputs:
- output: bfloat16 [16, 577, 1024], P(('dp', 'row'), None, 'col')
- grad_tokens: float32 [16, 577, 1024], P(('dp', 'row'), None, 'col')
- grad_w_qkv: float32 [1024, 3, 1024], P('row', None, 'col')
- grad_b_qv: float32 [2, 1024], P(None, 'col')
- grad_w_out: float32 [1024, 1024], P('row', 'col')
- grad_b_out: float32 [1024], P('col')
- grad_g_one: float32 [1024], P('col')
- grad_c_one: float32 [1024], P('col')
- grad_w_up: float32 [1024, 4096], P('row', 'col')
- grad_b_up: float32 [4096], P('col')
- grad_w_down: float32 [4096, 1024], P('row', 'col')
- grad_b_down: float32 [1024], P('col')
- grad_g_two: float32 [1024], P('col')
- grad_c_two: float32 [1024], P('col')
The draws below stay inside these ranges and needn't reach their ends.
All inputs are finite; a program needn't handle non-finite values.
Results may differ from the reference program's by a relative error of at most 0.01.
Values may be sent and summed in bfloat16 or wider, within the bound.
No kernel may reach another device: no remote copies, remote signals or barrier semaphores. Data moves between devices by JAX's collectives and lax.ppermute only.
A program may use at most 128 MiB of HBM per device.

```python
import jax
import jax.numpy as jnp
from jax import lax

D = 1024
H = 16
DH = 64
FF = 4096
SEQ = 577
IMAGES = 16


def block_scale(rng, shape, shards, smallest, top_value):
    level, own = 1.0, jax.random.fold_in(rng, 6)
    for dim, shards_of in shards:
        steps = jnp.exp(jax.random.uniform(jax.random.fold_in(own, dim), (shards_of,), jnp.float32, smallest / len(shards), top_value / len(shards)))
        level = level * jnp.repeat(steps, shape[dim] // shards_of).reshape([-1 if axis == dim else 1 for axis in range(len(shape))])
    return level


def noise(stream_key, shape, spread, most, shards=(), kind=jnp.bfloat16):
    level = block_scale(stream_key, shape, shards, -0.22, 0.18) if shards else 1.0
    array = jax.random.normal(stream_key, shape, jnp.float32) * spread * level
    return jnp.minimum(jnp.maximum(array, -most), most).astype(kind)


def setup_inputs(seed: int = 0) -> dict:
    keys = jax.random.split(jax.random.key(seed), 15)
    tokens = noise(keys[0], (IMAGES, SEQ, D), 1.0, 6.0, ((0, 8), (2, 4)))
    cotangent = noise(keys[1], (IMAGES, SEQ, D), 1.0, 6.0, ((0, 8), (2, 4)))
    w_qkv = noise(keys[2], (D, 3, D), D ** -0.5, 0.1875, ((0, 4), (2, 4)))
    b_qv = noise(keys[3], (2, D), 0.5, 3.0, ((1, 4),), jnp.float32)
    w_out = noise(keys[4], (D, D), (D // 16) ** -0.5, 0.75, ((0, 4), (1, 4)))
    b_out = noise(keys[5], (D,), 0.5, 3.0, ((0, 4),), jnp.float32)
    g_one = jnp.clip(1.0 + 0.18 * jax.random.normal(keys[6], (D,), jnp.float32), 0.1, 1.9)
    c_one = noise(keys[7], (D,), 0.5, 3.0, ((0, 4),), jnp.float32)
    w_up = noise(keys[8], (D, FF), D ** -0.5, 0.1875, ((0, 4), (1, 4)))
    b_up = noise(keys[9], (FF,), 0.5, 3.0, ((0, 4),), jnp.float32)
    w_down = noise(keys[10], (FF, D), FF ** -0.5, 0.09375, ((0, 4), (1, 4)))
    b_down = noise(keys[11], (D,), 0.5, 3.0, ((0, 4),), jnp.float32)
    g_two = jnp.clip(1.0 + 0.18 * jax.random.normal(keys[12], (D,), jnp.float32), 0.1, 1.9)
    c_two = noise(keys[13], (D,), 0.5, 3.0, ((0, 4),), jnp.float32)
    return dict(tokens=tokens, cotangent=cotangent, w_qkv=w_qkv, b_qv=b_qv, w_out=w_out, b_out=b_out, g_one=g_one, c_one=c_one, w_up=w_up, b_up=b_up, w_down=w_down, b_down=b_down, g_two=g_two, c_two=c_two)


@jax.custom_vjp
def low(v):
    return lax.optimization_barrier(v.astype(jnp.bfloat16)).astype(jnp.float32)

@jax.custom_vjp
def low_back(v):
    return v

def low_keep(v):
    return (low(v), None)

def low_pass(kept, grad):
    return (grad,)

def back_keep(v):
    return (v, None)

def back_low(kept, grad):
    return (low(grad),)
low.defvjp(low_keep, low_pass)
low_back.defvjp(back_keep, back_low)
HIGH = lax.Precision.HIGHEST

def norm_rows(values, gain, shift):
    mean = lax.optimization_barrier(jnp.mean(values, axis=-1, keepdims=True))
    second = lax.optimization_barrier(jnp.mean(values * values, axis=-1, keepdims=True))
    scale = lax.rsqrt(second - mean * mean + 1e-06)
    return (values - mean) * scale * gain + shift

def forward(image, params):
    w_qkv, b_qv, w_out, b_out, g_one, c_one, w_up, b_up, w_down, b_down, g_two, c_two = params
    normed = low(norm_rows(image, g_one, c_one))
    bias = jnp.stack([b_qv[0], jnp.zeros_like(b_qv[0]), b_qv[1]])
    packed = jnp.einsum('td,dkh->tkh', normed, w_qkv, precision=HIGH) + bias
    packed = low(low_back(packed))
    heads = packed.reshape(SEQ, 3, H, DH)
    query = heads[:, 0]
    key = heads[:, 1]
    value = heads[:, 2]
    scores = low_back(jnp.einsum('qhe,khe->hqk', query, key, precision=HIGH) * DH ** (-0.5))
    probs = jax.nn.softmax(scores, axis=-1)
    mixed = jnp.einsum('hqk,khe->qhe', low(probs), value, precision=HIGH).reshape(SEQ, D)
    mixed = low(low_back(mixed))
    branch = low_back(jnp.dot(mixed, w_out, precision=HIGH) + b_out)
    middle = image + branch
    normed_two = low(norm_rows(middle, g_two, c_two))
    inner = low_back(jnp.dot(normed_two, w_up, precision=HIGH) + b_up)
    hidden = low(jax.nn.gelu(inner, approximate=False))
    branch_two = low_back(jnp.dot(hidden, w_down, precision=HIGH) + b_down)
    return middle + branch_two

def reference(tokens, cotangent, w_qkv, b_qv, w_out, b_out, g_one, c_one, w_up, b_up, w_down, b_down, g_two, c_two):
    params = (w_qkv.astype(jnp.float32), b_qv.astype(jnp.float32), w_out.astype(jnp.float32), b_out.astype(jnp.float32), g_one.astype(jnp.float32), c_one.astype(jnp.float32), w_up.astype(jnp.float32), b_up.astype(jnp.float32), w_down.astype(jnp.float32), b_down.astype(jnp.float32), g_two.astype(jnp.float32), c_two.astype(jnp.float32))

    def one_image(totals, pair):
        image, cot = pair
        result, pull = jax.vjp(forward, image.astype(jnp.float32), params)
        grad_image, grad_params = pull(cot.astype(jnp.float32))
        totals = jax.tree.map(jnp.add, totals, grad_params)
        return (totals, (result.astype(jnp.bfloat16), grad_image))
    zeros = jax.tree.map(jnp.zeros_like, params)
    totals, (outputs, grad_tokens) = lax.scan(one_image, zeros, (tokens, cotangent))
    return (outputs, grad_tokens, totals[0], totals[1], totals[2], totals[3], totals[4], totals[5], totals[6], totals[7], totals[8], totals[9], totals[10], totals[11])
```

```python
from functools import partial

import jax
import jax.numpy as jnp
from jax import lax
from jax.experimental import pallas as pl
from jax.experimental.pallas import tpu as pltpu
from jax.sharding import Mesh
from jax.sharding import PartitionSpec as P

DH = 64
EPSILON = 1e-06
BF = jnp.bfloat16
F32 = jnp.float32
SWAP = ((0, 1), (1, 0))
MASKED = -1e30


def dot(a, b, ca, cb):
    return lax.dot_general(a, b, (((ca,), (cb,)), ((), ())), preferred_element_type=F32)


def attend_kernel(heads, packed_ref, bias_ref, mixed_ref, lse_ref):
    width = heads * DH
    bias = bias_ref[...]
    for h in range(heads):
        at = slice(h * DH, (h + 1) * DH)
        query = packed_ref[0, :, h * DH : (h + 1) * DH] * BF(DH**-0.5)
        key = packed_ref[0, :, width + h * DH : width + (h + 1) * DH]
        value = packed_ref[0, :, 2 * width + h * DH : 2 * width + (h + 1) * DH]
        scores = dot(key, query, 1, 1) + bias
        highest = jnp.max(scores, 0, keepdims=True)
        exponent = jnp.exp(scores - highest)
        total = jnp.sum(exponent, 0, keepdims=True)
        probs = (exponent * (1.0 / total)).astype(BF)
        mixed_ref[0, :, at] = dot(probs, value, 0, 0).astype(BF)
        lse_ref[0, h : h + 1, :] = highest + jnp.log(total)


def attend(packed, bias, heads):
    images, length, wide = packed.shape
    width = heads * DH
    return pl.pallas_call(
        partial(attend_kernel, heads),
        grid=(images,),
        in_specs=[
            pl.BlockSpec((1, length, wide), lambda i: (i, 0, 0)),
            pl.BlockSpec((length, 1), lambda i: (0, 0)),
        ],
        out_specs=[
            pl.BlockSpec((1, length, width), lambda i: (i, 0, 0)),
            pl.BlockSpec((1, heads, length), lambda i: (i, 0, 0)),
        ],
        out_shape=[
            jax.ShapeDtypeStruct((images, length, width), BF),
            jax.ShapeDtypeStruct((images, heads, length), F32),
        ],
        cost_estimate=pl.CostEstimate(
            flops=4 * images * length * length * width,
            bytes_accessed=images * length * (wide + width) * 2,
            transcendentals=images * heads * length * length,
        ),
        name="attend",
    )(packed, bias)


def attend_back_kernel(heads, packed_ref, bias_ref, lse_ref, grad_ref, out_ref):
    width = heads * DH
    bias = bias_ref[...]
    for h in range(heads):
        query = packed_ref[0, :, h * DH : (h + 1) * DH] * BF(DH**-0.5)
        key = packed_ref[0, :, width + h * DH : width + (h + 1) * DH]
        value = packed_ref[0, :, 2 * width + h * DH : 2 * width + (h + 1) * DH]
        grad = grad_ref[0, :, h * DH : (h + 1) * DH]
        scores = dot(key, query, 1, 1) + bias
        probs = jnp.exp(scores - lse_ref[0, h : h + 1, :])
        grad_probs = dot(value, grad, 1, 1)
        delta = jnp.sum(probs * grad_probs, 0, keepdims=True)
        grad_scores = (probs * (grad_probs - delta)).astype(BF)
        grad_query = dot(grad_scores, key, 0, 0) * (DH**-0.5)
        grad_key = dot(grad_scores, query, 1, 0)
        grad_value = dot(probs.astype(BF), grad, 1, 0)
        out_ref[0, :, h * DH : (h + 1) * DH] = grad_query.astype(BF)
        out_ref[0, :, width + h * DH : width + (h + 1) * DH] = grad_key.astype(BF)
        out_ref[0, :, 2 * width + h * DH : 2 * width + (h + 1) * DH] = grad_value.astype(BF)


def attend_back(packed, bias, lse, grad, heads):
    images, length, wide = packed.shape
    width = heads * DH
    return pl.pallas_call(
        partial(attend_back_kernel, heads),
        grid=(images,),
        in_specs=[
            pl.BlockSpec((1, length, wide), lambda i: (i, 0, 0)),
            pl.BlockSpec((length, 1), lambda i: (0, 0)),
            pl.BlockSpec((1, heads, length), lambda i: (i, 0, 0)),
            pl.BlockSpec((1, length, width), lambda i: (i, 0, 0)),
        ],
        out_specs=pl.BlockSpec((1, length, wide), lambda i: (i, 0, 0)),
        out_shape=jax.ShapeDtypeStruct((images, length, wide), BF),
        cost_estimate=pl.CostEstimate(
            flops=10 * images * length * length * width,
            bytes_accessed=images * length * (2 * wide + width) * 2,
            transcendentals=images * heads * length * length,
        ),
        name="attend_back",
    )(packed, bias, lse, grad)


def xor_slots(parts, bits):
    low, high = bits % 2 == 1, bits // 2 == 1
    a = [jnp.where(low, parts[s ^ 1], parts[s]) for s in range(4)]
    return [jnp.where(high, a[s ^ 2], a[s]) for s in range(4)]


def pairs_of(step, back):
    pairs = []
    for k in range(2):
        for z in range(4):
            piece = z ^ step
            native, spread = (k * 4 + z), ((piece % 2) * 4 + 2 * k + piece // 2)
            pairs.append((spread, native) if back else (native, spread))
    return pairs


def to_images(pieces, place):
    z, slot = place["z"], place["slot"]
    sends = xor_slots(pieces, z)
    received = [lax.ppermute(sends[j], ("k", "col"), pairs_of(j, False)) for j in range(4)]
    return xor_slots(received, slot)


def from_images(blocks, place):
    z, slot = place["z"], place["slot"]
    sends = xor_slots(blocks, slot)
    received = [lax.ppermute(sends[j], ("k", "col"), pairs_of(j, True)) for j in range(4)]
    return xor_slots(received, z)


def gather_tokens(half):
    sibling = lax.ppermute(half, "k", SWAP)
    far = lax.ppermute(half, "x", SWAP)
    far_sibling = lax.ppermute(far, "k", SWAP)
    return jnp.stack([half, sibling, far, far_sibling])


def reduce_tokens(partial_sums):
    low = partial_sums[:, 1].astype(BF)
    recv = lax.ppermute(low, "k", SWAP)
    far = (partial_sums[1, 0] + recv[1].astype(F32)).astype(BF)
    far = lax.ppermute(far, "x", SWAP)
    return partial_sums[0, 0] + recv[0].astype(F32) + far.astype(F32)


def norm_forward(values, gain, shift):
    width = values.shape[-1]
    mean = jnp.sum(values, -1, keepdims=True) / width
    second = jnp.sum(values * values, -1, keepdims=True) / width
    scale = lax.rsqrt(second - mean * mean + EPSILON)
    centred = (values - mean) * scale
    return centred, scale, (centred * gain + shift).astype(BF)


def norm_backward(grad, centred, scale, gain):
    width = grad.shape[-1]
    scaled = grad * gain
    first = jnp.sum(scaled, -1, keepdims=True) / width
    second = jnp.sum(scaled * centred, -1, keepdims=True) / width
    grad_in = scale * (scaled - first - centred * second)
    return grad_in, jnp.sum(grad * centred, 0), jnp.sum(grad, 0)


def pick(parts, bit):
    return jnp.where(bit == 1, parts[1], parts[0])


def shards(
    tokens, cotangent, w_qkv, b_qv, w_out, b_out, g_one, c_one,
    w_up, b_up, w_down, b_down, g_two, c_two,
):
    images, length, block = tokens.shape
    cols = lax.axis_size("col")
    rows = lax.axis_size("y") * 2
    width = block * cols
    heads = cols * block // (4 * DH)
    ffb = w_up.shape[1]
    ffq = ffb // 4
    half = -(-length // 16) * 8
    padded = 2 * half
    x, k, z = lax.axis_index("x"), lax.axis_index("k"), lax.axis_index("col")
    part = 2 * x + k
    place = {"z": z, "slot": (z % 2) * 2 + k}

    def halves(a):
        a = jnp.pad(a, ((0, 0), (0, padded - length), (0, 0)))
        return [a[i, h * half : (h + 1) * half] for i in range(2) for h in range(2)]

    small = jnp.concatenate([b_qv[0], b_qv[1], b_out, g_one, c_one, b_down, g_two, c_two, b_up])
    small = lax.all_gather(small, "col", axis=0, tiled=False)
    names = [small[:, i * block : (i + 1) * block] for i in range(8)]
    b_q_all, b_v_all = names[0], names[1]
    b_out_all, gain_one, shift_one, b_down_all, gain_two, shift_two = [
        v.reshape(width) for v in names[2:]
    ]
    b_q_own, b_v_own = [
        lax.dynamic_slice_in_dim(v, part * DH, DH, axis=1).reshape(heads * DH)
        for v in (b_q_all, b_v_all)
    ]
    bias_qkv = jnp.concatenate([b_q_own, jnp.zeros_like(b_q_own), b_v_own])
    b_up_own = lax.dynamic_slice_in_dim(small[:, 8 * block :], part * ffq, ffq, axis=1).reshape(-1)

    qkv_t = jnp.transpose(w_qkv, (1, 2, 0)).reshape(3, 4, DH, block)
    out_4 = w_out.reshape(4, DH, block)
    up_4 = jnp.moveaxis(w_up.reshape(block, 4, ffq), 1, 0)
    down_4 = w_down.reshape(4, ffq, block)

    def quarter(kk):
        q = 2 * x + kk
        at = lambda a, axis: lax.dynamic_index_in_dim(a, q, axis, keepdims=False)
        first = jnp.concatenate([at(qkv_t, 1).reshape(3 * DH, block), at(out_4, 0)])
        second = jnp.concatenate([at(up_4, 0), at(down_4, 0)])
        return first, second

    def spread_weights(mine, give):
        got = lax.ppermute(give, "k", SWAP)
        both = jnp.stack([jnp.where(k == 0, mine, got), jnp.where(k == 0, got, mine)])
        return lax.all_gather(both, ("y", "col"), axis=0, tiled=False).reshape(
            rows // 2, cols, 2, *mine.shape
        )

    (mine_1, mine_2), (give_1, give_2) = quarter(k), quarter(1 - k)
    all_1 = spread_weights(mine_1, give_1)
    all_2 = spread_weights(mine_2, give_2)
    by_row = lambda a: jnp.transpose(a, (0, 2, 3, 1, 4)).reshape(-1, cols * a.shape[-1])
    full_qkv = jnp.transpose(
        all_1[:, :, :, : 3 * DH].reshape(rows // 2, cols, 2, 3, DH, block), (3, 1, 4, 0, 2, 5)
    ).reshape(3 * heads * DH, width)
    full_out = by_row(all_1[:, :, :, 3 * DH :])
    full_up = by_row(all_2[:, :, :, :block])
    full_down = by_row(all_2[:, :, :, block:])

    start_x = jnp.concatenate(to_images(halves(tokens), place), axis=1).astype(F32)
    grad_out = jnp.concatenate(to_images(halves(cotangent), place), axis=1)
    centred_one, scale_one, normed_one = norm_forward(start_x, gain_one, shift_one)
    wide_one = gather_tokens(normed_one).reshape(2 * padded, width)
    packed = (dot(wide_one, full_qkv, 1, 1) + bias_qkv).astype(BF)
    packed = packed.reshape(2, padded, 3 * heads * DH)
    at_half, at_row = jnp.arange(padded) // half, jnp.arange(padded) % half
    token = jnp.where(k == 0, at_half, 1 - at_half) * half + at_row
    bias = jnp.where(token < length, 0.0, MASKED).astype(F32)[:, None]
    mixed, lse = attend(packed, bias, heads)
    mixed = mixed.reshape(2 * padded, heads * DH)
    split = lambda a: a.reshape(2, 2, half, width)
    middle = start_x + (reduce_tokens(split(dot(mixed, full_out, 1, 0))) + b_out_all)
    centred_two, scale_two, normed_two = norm_forward(middle, gain_two, shift_two)
    wide_two = gather_tokens(normed_two).reshape(2 * padded, width)
    low_two = gather_tokens(grad_out).reshape(2 * padded, width)
    inner = dot(wide_two, full_up, 1, 0) + b_up_own
    hidden, gelu_pull = jax.vjp(partial(jax.nn.gelu, approximate=False), inner)
    hidden = hidden.astype(BF)
    down_sum = reduce_tokens(split(dot(hidden, full_down, 1, 0)))
    output = (middle + (down_sum + b_down_all)).astype(BF)

    def native(a):
        blocks = [a[:, i * block : (i + 1) * block] for i in range(4)]
        p = from_images(blocks, place)
        return jnp.stack(
            [jnp.concatenate([p[2 * i], p[2 * i + 1]], 0)[:length] for i in range(2)]
        )

    output = native(output)

    grad_inner = gelu_pull(dot(low_two, full_down, 1, 1))[0]
    low_inner = grad_inner.astype(BF)
    term_down = dot(hidden, low_two, 0, 0)
    term_up = dot(wide_two, low_inner, 0, 0)
    grad_two = reduce_tokens(split(dot(low_inner, full_up, 1, 1)))
    back_two, gain_two_grad, shift_two_grad = norm_backward(
        grad_two, centred_two, scale_two, gain_two
    )
    grad_middle = grad_out.astype(F32) + back_two
    low_one = grad_middle.astype(BF)
    wide_done = gather_tokens(low_one).reshape(2 * padded, width)
    term_out = dot(mixed, wide_done, 0, 0)
    grad_mixed = dot(wide_done, full_out, 1, 1).astype(BF).reshape(2, padded, heads * DH)
    low_packed = attend_back(packed, bias, lse, grad_mixed, heads).reshape(2 * padded, -1)
    term_qkv = dot(low_packed, wide_one, 0, 0)
    grad_one = reduce_tokens(split(dot(low_packed, full_qkv, 1, 0)))
    back_one, gain_one_grad, shift_one_grad = norm_backward(
        grad_one, centred_one, scale_one, gain_one
    )
    grad_tokens = native((grad_middle + back_one).astype(BF)).astype(F32)

    def per_block(a):
        a = a.reshape(rows // 2, 2, a.shape[0] // rows, cols, block)
        return jnp.transpose(a, (0, 3, 1, 2, 4))

    qkv_blocks = jnp.transpose(
        term_qkv.astype(BF).reshape(3, cols, DH, rows // 2, 2, block), (3, 1, 4, 0, 2, 5)
    ).reshape(rows // 2, cols, 2, 3 * DH, block)
    terms_1 = jnp.concatenate([qkv_blocks, per_block(term_out.astype(BF))], 3)
    terms_2 = jnp.concatenate([per_block(term_up.astype(BF)), per_block(term_down.astype(BF))], 3)

    def owned(terms):
        terms = terms.reshape(rows // 2 * cols * 2, *terms.shape[3:])
        both = lax.psum_scatter(terms, ("y", "col"), scatter_dimension=0, tiled=True)
        got = lax.ppermute(jnp.where(k == 0, both[1], both[0]), "k", SWAP)
        mine = jnp.where(k == 0, both[0], both[1])
        near = jnp.stack([jnp.where(k == 0, mine, got), jnp.where(k == 0, got, mine)])
        far = lax.ppermute(near, "x", SWAP)
        four = jnp.concatenate([jnp.where(x == 0, near, far), jnp.where(x == 0, far, near)])
        if lax.axis_size("rep") > 1:
            four = lax.psum(four.astype(F32), "rep")
        return four.astype(F32)

    four_2 = owned(terms_2)
    four_1 = owned(terms_1)
    grad_wup = jnp.moveaxis(four_2[:, :block], 0, 1).reshape(block, ffb)
    grad_wdown = four_2[:, block:].reshape(ffb, block)
    grad_qkv = jnp.transpose(
        four_1[:, : 3 * DH].reshape(4, 3, DH, block), (3, 1, 0, 2)
    ).reshape(block, 3, block)
    grad_wout = four_1[:, 3 * DH :].reshape(4 * DH, block)

    def own_slots(vector, n):
        blank = jnp.zeros((cols, 4, n), F32)
        return lax.dynamic_update_slice_in_dim(
            blank, vector.reshape(cols, 1, n), part, axis=1
        ).reshape(cols, 4 * n)

    sum_packed = jnp.sum(low_packed.astype(F32), 0).reshape(3, heads * DH)
    by_col = lambda v: v.reshape(cols, block)
    sums = jnp.concatenate(
        [
            own_slots(sum_packed[0], DH),
            own_slots(sum_packed[2], DH),
            by_col(jnp.sum(low_one.astype(F32), 0)),
            by_col(gain_one_grad),
            by_col(shift_one_grad),
            by_col(jnp.sum(grad_out.astype(F32), 0)),
            by_col(gain_two_grad),
            by_col(shift_two_grad),
            own_slots(jnp.sum(low_inner.astype(F32), 0), ffq),
        ],
        1,
    )
    sums = lax.psum(sums, ("rep", "x", "y", "k", "col"))
    mine = lax.dynamic_index_in_dim(sums, z, 0, keepdims=False)
    vec = [mine[i * block : (i + 1) * block] for i in range(8)]
    return (
        output, grad_tokens, grad_qkv, jnp.stack([vec[0], vec[1]]), grad_wout, vec[2], vec[3], vec[4],
        grad_wup, mine[8 * block :], grad_wdown, vec[5], vec[6], vec[7],
    )


def solution(mesh):
    dp, row, col = (mesh.shape[n] for n in ("dp", "row", "col"))
    grid = Mesh(
        mesh.devices.reshape(dp // 2, 2, row // 2, 2, col), ("rep", "x", "y", "k", "col")
    )
    batch = P(("rep", "x", "y", "k"), None, "col")
    rows = ("y", "k")
    weight = P(rows, "col")
    one = P("col")
    return jax.shard_map(
        shards,
        mesh=grid,
        in_specs=(
            batch, batch, P(rows, None, "col"), P(None, "col"), weight, one, one, one,
            weight, one, weight, one, one, one,
        ),
        out_specs=(
            batch, batch, P(rows, None, "col"), P(None, "col"), weight, one, one, one,
            weight, one, weight, one, one, one,
        ),
        check_vma=False,
    )
```
